512 devices in a mesh: dp: 64 (over z, y_hi, core), stat: 8 (over x, y_lo).
Axes of the slice: x: 4, y: 8 (y_hi: 4, y_lo: 2; y = y_hi * 2 + y_lo), z: 8, core: 2. Of those that a mesh axis runs over, the one named last changes fastest.
Arguments:
- activations: bfloat16 [65536, 8192], P('dp'), may hold values from -16 to 16
- out_grads: bfloat16 [65536, 1024], P('dp', 'stat'), may hold values from -0.0234375 to 0.0234375
- stat_old: float32 [192, 128, 128], P('dp'), may hold values from -0.24 to 0.24
- pattern: int32 [192, 2], replicated, may hold values from 0 to 63, as said below
- holders: int32 [192], replicated, may hold values from 0 to 63, as said below
Outputs:
- direction: float32 [8192, 1024], P('dp', 'stat')
- statistics: float32 [192, 128, 128], P('dp', 'stat')
The draws below stay inside these ranges and needn't reach their ends.
Inputs may be any that keep to these rules, and one draw needn't show every extreme that they name: `pattern`: every diagonal pair (a, a) for a in 0 to 63 appears exactly once; every other entry has different row and column blocks; half of those are band pairs (column block next to the row block, cyclically), the rest reach anywhere. `holders`: every dp index holds exactly 3 entries; the diagonal entry (a, a) is held by the dp index whose weight rows contain row a * 128.
All inputs are finite; a program needn't handle non-finite values.
Results may differ from the reference program's by a relative error of at most 0.003.
Values may be sent and summed in bfloat16 or wider, within the bound.
No kernel may reach another device: no remote copies, remote signals or barrier semaphores. Data moves between devices by JAX's collectives and lax.ppermute only.
A program may use at most 192 MiB of HBM per device.

```python
import jax
import jax.numpy as jnp
from jax import lax

D = 8192
BLOCK = 128
ITERS = 5
NB = 64
NBLK = 192
COLS = 1024
TOKENS = 65536
N_DP = 64


def pattern_tables(key):
    base = jax.random.fold_in(key, 7)
    key_start, key_far, key_perm, key_side = jax.random.split(base, 4)
    extra = NBLK - NB
    starts = jax.random.randint(key_start, (extra,), 0, NB)
    far_off = jax.random.randint(key_far, (extra,), 1, NB)
    side = jax.random.randint(key_side, (extra,), 0, 2)
    near_off = jnp.where(side == 0, 1, NB - 1)
    offsets = jnp.where(jnp.arange(extra) < extra // 2, near_off, far_off)
    ends = (starts + offsets) % NB
    diag = jnp.arange(NB, dtype=jnp.int32)
    row_blocks = jnp.concatenate([diag, starts.astype(jnp.int32)])
    col_blocks = jnp.concatenate([diag, ends.astype(jnp.int32)])
    holder_ids = jnp.concatenate([diag // (NB // N_DP), jnp.arange(extra, dtype=jnp.int32) % N_DP])
    perm = jax.random.permutation(key_perm, NBLK)
    pairs = jnp.stack([row_blocks, col_blocks], axis=1)[perm]
    return (pairs.astype(jnp.int32), holder_ids[perm].astype(jnp.int32))


def draw_pattern(key, part):
    return pattern_tables(key)[0]


def draw_holders(key, part):
    return pattern_tables(key)[1]


def spiked(entries, own_key, source, target, shards_of, factor):
    owner, partner = [(jnp.arange(entries.shape[position]) // (entries.shape[position] // shards_of)).reshape([-1 if axis == position else 1 for axis in range(entries.ndim)]) for position in (source, target)]
    chosen = jax.random.permutation(own_key, shards_of)[partner]
    strong = (owner == chosen) | (owner == (partner + shards_of // 2) % shards_of)
    return jnp.where(strong, factor * entries, entries)


def level_of(own_key, shape, pieces, least, largest):
    gain = 1.0
    for axis_at, shards_of in pieces:
        heights = jax.random.uniform(jax.random.fold_in(jax.random.fold_in(own_key, 6), axis_at), (shards_of,), jnp.float32, least / len(pieces), largest / len(pieces))
        gain = gain * jnp.repeat(jnp.exp(heights), shape[axis_at] // shards_of).reshape((-1,) + (1,) * (len(shape) - 1 - axis_at))
    return gain


def bell_draw(rng, extent, spread, limit, cuts=(), held_as=jnp.bfloat16):
    values = jax.random.normal(rng, extent, jnp.float32) * spread
    if len(cuts) > 0:
        values = level_of(rng, extent, cuts, -0.22, 0.18) * values
    return jnp.clip(values, min=-limit, max=limit).astype(held_as)


def noise_with(key, extent, spread, most, pieces, heavy, kind=jnp.bfloat16):
    values = spread * jax.random.normal(key, extent, jnp.float32)
    if pieces:
        values = values * level_of(key, extent, pieces, -0.22, 0.18)
    return jnp.clip(spiked(values, jax.random.fold_in(key, 3), *heavy), -most, most).astype(kind)


def setup_inputs(seed: int = 0) -> dict:
    key_of = jax.random.split(jax.random.key(seed), 6)
    activations = noise_with(key_of[0], (TOKENS, D), 1.0, 16.0, ((0, 64),), (0, 1, 64, 4.0))
    out_grads = bell_draw(key_of[1], (TOKENS, COLS), TOKENS ** -0.5, 0.0234375, ((0, 64), (1, 8)))
    stat_old = bell_draw(key_of[2], (NBLK, BLOCK, BLOCK), 0.04, 0.24, ((0, 64),), jnp.float32)
    pattern = draw_pattern(jax.random.fold_in(key_of[5], 71), 0)
    holders = draw_holders(jax.random.fold_in(key_of[5], 71), 0)
    return dict(activations=activations, out_grads=out_grads, stat_old=stat_old, pattern=pattern, holders=holders)


beta_stat = 0.6
damping = 0.75

def inverse_root(matrix):
    size = matrix.shape[0]
    eye = jnp.eye(size, dtype=matrix.dtype)
    sym = 0.5 * (matrix + matrix.T) + damping * eye
    scale = jnp.sqrt(jnp.sum(sym * sym))
    current = sym / scale
    result = eye
    for sweep in range(ITERS):
        factor = (5.0 * eye - current) * 0.25
        result = jnp.dot(result, factor, precision=lax.Precision.HIGHEST)
        square = jnp.dot(factor, factor, precision=lax.Precision.HIGHEST)
        fourth = jnp.dot(square, square, precision=lax.Precision.HIGHEST)
        current = jnp.dot(fourth, current, precision=lax.Precision.HIGHEST)
    return result * scale ** (-0.25)

def reference(activations, out_grads, stat_old, pattern, holders):
    grad = lax.dot_general(activations, out_grads, (((0,), (0,)), ((), ())), preferred_element_type=jnp.float32)
    grad_b = grad.astype(jnp.bfloat16)
    order = jnp.argsort(holders, stable=True)
    row_blocks = pattern[order, 0]
    col_blocks = pattern[order, 1]

    def gram_of(pair):
        first = lax.dynamic_slice_in_dim(grad_b, (pair[0] * BLOCK).astype(jnp.int32), BLOCK, 0)
        second = lax.dynamic_slice_in_dim(grad_b, (pair[1] * BLOCK).astype(jnp.int32), BLOCK, 0)
        return lax.dot_general(first, second, (((1,), (1,)), ((), ())), preferred_element_type=jnp.float32)
    grams = lax.map(gram_of, (row_blocks, col_blocks)) / COLS
    statistics = beta_stat * stat_old + (1.0 - beta_stat) * grams
    panel_ids = jnp.arange(NB, dtype=jnp.int32)
    match = (row_blocks[None, :] == panel_ids[:, None]) & (col_blocks[None, :] == panel_ids[:, None])
    where_diag = jnp.argmax(match.astype(jnp.int32), axis=1)
    diagonal = statistics[where_diag]
    roots = lax.map(inverse_root, diagonal)
    stacked = grad_b.reshape(NB, BLOCK, COLS).astype(jnp.float32)
    direction = jnp.einsum('irs,isc->irc', roots, stacked, precision=lax.Precision.HIGHEST).reshape(D, COLS)
    return (direction, statistics)
```

```python
import jax
import jax.numpy as jnp
from jax import lax
from jax.sharding import PartitionSpec as P

ITERS = 5
beta_stat = 0.6
damping = 0.75

NZ, NY, NC = 8, 4, 2
Z_GROUPS = [[z * NY * NC + r for z in range(NZ)] for r in range(NY * NC)]
Y_GROUPS = [[(z * NY + y) * NC + c for y in range(NY)] for z in range(NZ) for c in range(NC)]

f32 = jnp.float32
bf16 = jnp.bfloat16
HI = lax.Precision.HIGHEST


def inverse_root(matrix):
    size = matrix.shape[0]
    eye = jnp.eye(size, dtype=matrix.dtype)
    sym = 0.5 * (matrix + matrix.T) + damping * eye
    scale = jnp.sqrt(jnp.sum(sym * sym))
    current = sym / scale
    result = eye
    for sweep in range(ITERS):
        factor = (5.0 * eye - current) * 0.25
        if sweep == 0:
            result = factor
        else:
            result = jnp.dot(result, factor, precision=HI)
        if sweep < ITERS - 1:
            square = jnp.dot(factor, factor, precision=HI)
            fourth = jnp.dot(square, square, precision=HI)
            current = jnp.dot(fourth, current, precision=HI)
    return result * scale ** (-0.25)


def exchange(x, axis, groups=None):
    return lax.all_to_all(x, axis, 0, 0, axis_index_groups=groups, tiled=True)


def tables(pattern, holders, position, held, n_dp):
    rows, cols = pattern[:, 0], pattern[:, 1]
    entries = jnp.arange(holders.shape[0], dtype=jnp.int32)
    off = rows != cols
    same = (holders[None, :] == holders[:, None]) & (entries[None, :] < entries[:, None])
    within = jnp.sum(same.astype(jnp.int32), axis=1)
    rank = jnp.sum((same & off[None, :]).astype(jnp.int32), axis=1)
    dests = jnp.arange(n_dp, dtype=jnp.int32)
    mine = off[None, :] & (holders[None, :] == dests[:, None])
    needs = [dests, dests]
    for m in range(held - 1):
        hit = (mine & (rank[None, :] == m)).astype(jnp.int32)
        needs.append(jnp.sum(hit * rows[None, :], axis=1))
        needs.append(jnp.sum(hit * cols[None, :], axis=1))
    diag_slot = jnp.sum(jnp.where((~off) & (holders == position), within, 0))
    return needs, diag_slot


def per_device(activations, out_grads, stat_old, pattern, holders):
    position = lax.axis_index("dp")
    stat_pos = lax.axis_index("stat")
    n_stat = lax.axis_size("stat")
    n_dp = NZ * NY * NC
    block = stat_old.shape[2]
    held = stat_old.shape[0]
    width = out_grads.shape[1]
    rows = activations.shape[1]
    panels = rows // block
    half = panels // NC
    zr = block // NZ
    yr = zr // NY
    share = block // n_stat
    core = position % NC

    partial = lax.dot_general(
        activations, out_grads, (((0,), (0,)), ((), ())), preferred_element_type=f32
    ).reshape(NC, half * block, width)
    give = lax.dynamic_index_in_dim(partial, 1 - core, 0, keepdims=False)
    keep = lax.dynamic_index_in_dim(partial, core, 0, keepdims=False)
    got = lax.ppermute(give, "dp", [(i, i ^ 1) for i in range(n_dp)])
    pair = (keep + got).reshape(half, NZ, zr, width).transpose(1, 0, 2, 3)
    pair = exchange(pair.astype(bf16).reshape(NZ, half * zr, width), "dp", Z_GROUPS)
    line = jnp.sum(pair.astype(f32), axis=0).reshape(half, NY, yr, width)
    line = line.transpose(1, 0, 2, 3).reshape(NY, half * yr, width)
    owned = jnp.sum(exchange(line, "dp", Y_GROUPS), axis=0)
    owned = owned.reshape(half, yr * width)

    needs, diag_slot = tables(pattern, holders, position, held, n_dp)
    high = owned.astype(bf16)
    low = (owned - high.astype(f32)).astype(bf16)
    local = jnp.arange(half, dtype=jnp.int32) + core * half
    sent = []
    for k, need in enumerate(needs):
        pick = (need[:, None] == local[None, :]).astype(bf16)
        sent.append(jnp.dot(pick, low if k == 1 else high, preferred_element_type=f32).astype(bf16))
    kinds = len(sent)
    sent = jnp.stack(sent, axis=1).reshape(n_dp, kinds * yr, width)
    came = exchange(sent, "dp").reshape(NZ * NY, NC, kinds, yr, width)
    came = (came[:, 0] + came[:, 1]).transpose(1, 0, 2, 3).reshape(kinds, block, width)

    def gram_of(a, b):
        return lax.dot_general(a, b, (((1,), (1,)), ((), ())), preferred_element_type=f32)

    diag = jnp.broadcast_to(gram_of(came[0], came[0])[None], (n_stat, block, block))
    others = [
        gram_of(came[2 + 2 * m], came[3 + 2 * m]).reshape(n_stat, share, block)
        for m in range(held - 1)
    ]
    grams = exchange(jnp.concatenate([diag] + others, axis=1), "stat")
    grams = jnp.sum(grams, axis=0) * ((1.0 - beta_stat) / (width * n_stat))

    old_diag = lax.dynamic_index_in_dim(stat_old, diag_slot, 0, keepdims=False)
    new_diag = beta_stat * old_diag + grams[:block]
    root = inverse_root(new_diag)
    grad = came[0].astype(f32) + came[1].astype(f32)
    direction = jnp.dot(root, grad, precision=HI)

    diag_rows = lax.dynamic_slice_in_dim(grams[:block], stat_pos * share, share, 0)
    slots = []
    for j in range(held):
        part = diag_rows
        for m in range(held - 1):
            here = (diag_slot != j) & (jnp.where(diag_slot < j, j - 1, j) == m)
            part = jnp.where(here, grams[block + m * share : block + (m + 1) * share], part)
        slots.append(part)
    old_rows = lax.dynamic_slice_in_dim(stat_old, stat_pos * share, share, 1)
    statistics = beta_stat * old_rows + jnp.stack(slots)
    return (direction, statistics)


def solution(mesh):
    placed = (P("dp", None), P("dp", "stat"), P("dp", None, None), P(), P())
    return jax.shard_map(
        per_device,
        mesh=mesh,
        in_specs=placed,
        out_specs=(P("dp", "stat"), P("dp", "stat", None)),
        check_vma=False,
    )
```

```python
import jax
import jax.numpy as jnp
from jax import lax
from jax.sharding import PartitionSpec as P

ITERS = 5
beta_stat = 0.6
damping = 0.75

NZ, NY, NC = 8, 4, 2
Z_GROUPS = [[z * NY * NC + r for z in range(NZ)] for r in range(NY * NC)]
Y_GROUPS = [[[(z * NY + y) * NC + c for y in range(NY)] for z in range(NZ)] for c in range(NC)]
QUADS = [
    [[(z * NY + y) * NC + c for z in range(p, NZ, 2)] for y in range(NY) for p in range(2)]
    for c in range(NC)
]
FIRST = Y_GROUPS[0] + QUADS[1]
SECOND = QUADS[0] + Y_GROUPS[1]
YC_GROUPS = [[z * NY * NC + r for r in range(NY * NC)] for z in range(NZ)]

f32 = jnp.float32
bf16 = jnp.bfloat16
HI = lax.Precision.HIGHEST


def inverse_root(matrix):
    size = matrix.shape[0]
    eye = jnp.eye(size, dtype=matrix.dtype)
    sym = 0.5 * (matrix + matrix.T) + damping * eye
    scale = jnp.sqrt(jnp.sum(sym * sym))
    current = sym / scale
    result = eye
    for sweep in range(ITERS):
        factor = (5.0 * eye - current) * 0.25
        if sweep == 0:
            result = factor
        else:
            result = jnp.dot(result, factor, precision=HI)
        if sweep < ITERS - 1:
            square = jnp.dot(factor, factor, precision=HI)
            fourth = jnp.dot(square, square, precision=HI)
            current = jnp.dot(fourth, current, precision=HI)
    return result * scale ** (-0.25)


def exchange(x, axis, groups=None):
    return lax.all_to_all(x, axis, 0, 0, axis_index_groups=groups, tiled=True)


def tables(pattern, holders, position, held, n_dp):
    rows, cols = pattern[:, 0], pattern[:, 1]
    entries = jnp.arange(holders.shape[0], dtype=jnp.int32)
    off = rows != cols
    same = (holders[None, :] == holders[:, None]) & (entries[None, :] < entries[:, None])
    within = jnp.sum(same.astype(jnp.int32), axis=1)
    rank = jnp.sum((same & off[None, :]).astype(jnp.int32), axis=1)
    dests = jnp.arange(n_dp, dtype=jnp.int32)
    mine = off[None, :] & (holders[None, :] == dests[:, None])
    needs = [dests, dests]
    for m in range(held - 1):
        hit = (mine & (rank[None, :] == m)).astype(jnp.int32)
        needs.append(jnp.sum(hit * rows[None, :], axis=1))
        needs.append(jnp.sum(hit * cols[None, :], axis=1))
    diag_slot = jnp.sum(jnp.where((~off) & (holders == position), within, 0))
    return needs, diag_slot


def per_device(activations, out_grads, stat_old, pattern, holders):
    position = lax.axis_index("dp")
    stat_pos = lax.axis_index("stat")
    n_stat = lax.axis_size("stat")
    n_dp = NZ * NY * NC
    block = stat_old.shape[2]
    held = stat_old.shape[0]
    width = out_grads.shape[1]
    rows = activations.shape[1]
    panels = rows // block
    quarter = panels // (2 * NC)
    yr = block // (NZ * NY)
    share = block // n_stat
    core = jnp.bitwise_and(position, NC - 1)

    def pair_sum(chunk):
        partial = lax.dot_general(
            activations[:, chunk * (rows // 2) : (chunk + 1) * (rows // 2)],
            out_grads,
            (((0,), (0,)), ((), ())),
            preferred_element_type=f32,
        )
        lower, upper = partial[: rows // 4], partial[rows // 4 :]
        give = jnp.where(core == 0, upper, lower)
        got = lax.ppermute(give, "dp", [(i, i ^ 1) for i in range(n_dp)])
        return jnp.where(core == 0, lower, upper) + got

    def spread(k):
        x = pair_sum(k).astype(bf16).reshape(quarter, NY, block // NY, width).transpose(1, 0, 2, 3)
        x = exchange(x.reshape(NY, quarter * block // NY, width), "dp", FIRST)
        return jnp.sum(x.astype(f32), axis=0).reshape(quarter, NY, 2 * yr, width)

    x = jnp.concatenate([spread(0), spread(1)]).transpose(1, 0, 2, 3)
    x = exchange(x.reshape(NY, 4 * quarter * yr, width), "dp", SECOND)
    x = jnp.sum(x, axis=0).reshape(2 * quarter, 2, yr, width)
    odd = jnp.bitwise_and(position // (NY * NC), 1)
    even_rows, odd_rows = x[:, 0], x[:, 1]
    got = lax.ppermute(
        jnp.where(odd == 0, odd_rows, even_rows),
        "dp",
        [(i, i ^ (NY * NC)) for i in range(n_dp)],
    )
    owned = (jnp.where(odd == 0, even_rows, odd_rows) + got).reshape(2 * quarter, yr * width)

    needs, diag_slot = tables(pattern, holders, position, held, n_dp)
    kinds = len(needs)
    needs = jnp.stack(needs, axis=1)
    mine = jnp.sum(jnp.where(jnp.arange(n_dp)[:, None] == position, needs, 0), axis=0)
    high = owned.astype(bf16)
    low = (owned - high.astype(f32)).astype(bf16)
    order = jnp.arange(2 * quarter, dtype=jnp.int32)
    local = jnp.where(order < quarter, order, order + (panels // 2 - quarter)) + core * quarter
    local = jnp.concatenate([local, local + panels])
    wanted = needs + jnp.where(jnp.arange(kinds) == 1, panels, 0)
    pick = (wanted[:, :, None] == local).astype(bf16).reshape(n_dp * kinds, 4 * quarter)
    sent = jnp.dot(pick, jnp.concatenate([high, low]), preferred_element_type=f32).astype(bf16)
    plane = NY * NC
    sent = exchange(sent.reshape(NZ, plane * kinds * yr, width), "dp", Z_GROUPS)
    sent = sent.reshape(NZ, plane, kinds * yr, width).transpose(1, 0, 2, 3)
    sent = exchange(sent.reshape(plane, NZ * kinds * yr, width), "dp", YC_GROUPS)
    came = sent.reshape(NY, NC, NZ, kinds, yr, width)
    came = came[:, 0] + came[:, 1]
    by_y = came.transpose(2, 0, 1, 3, 4).reshape(kinds, block, width)
    by_z = came.reshape(NY, NZ // 2, 2, kinds, yr, width).transpose(3, 1, 0, 2, 4, 5)
    by_z = by_z.reshape(kinds, block, width)
    came = jnp.where((jnp.bitwise_and(mine // quarter, 1) == 0)[:, None, None], by_y, by_z)

    def gram_of(a, b):
        return lax.dot_general(a, b, (((1,), (1,)), ((), ())), preferred_element_type=f32)

    diag = jnp.broadcast_to(gram_of(came[0], came[0])[None], (n_stat, block, block))
    others = [
        gram_of(came[2 + 2 * m], came[3 + 2 * m]).reshape(n_stat, share, block)
        for m in range(held - 1)
    ]
    grams = exchange(jnp.concatenate([diag] + others, axis=1), "stat")
    grams = jnp.sum(grams, axis=0) * ((1.0 - beta_stat) / (width * n_stat))

    old_diag = lax.dynamic_index_in_dim(stat_old, diag_slot, 0, keepdims=False)
    new_diag = beta_stat * old_diag + grams[:block]
    root = inverse_root(new_diag)
    grad = came[0].astype(f32) + came[1].astype(f32)
    direction = jnp.dot(root, grad, precision=HI)

    diag_rows = lax.dynamic_slice_in_dim(grams[:block], stat_pos * share, share, 0)
    slots = []
    for j in range(held):
        part = diag_rows
        for m in range(held - 1):
            here = (diag_slot != j) & (jnp.where(diag_slot < j, j - 1, j) == m)
            part = jnp.where(here, grams[block + m * share : block + (m + 1) * share], part)
        slots.append(part)
    old_rows = lax.dynamic_slice_in_dim(stat_old, stat_pos * share, share, 1)
    statistics = beta_stat * old_rows + jnp.stack(slots)
    return (direction, statistics)


def solution(mesh):
    placed = (P("dp", None), P("dp", "stat"), P("dp", None, None), P(), P())
    return jax.shard_map(
        per_device,
        mesh=mesh,
        in_specs=placed,
        out_specs=(P("dp", "stat"), P("dp", "stat", None)),
        check_vma=False,
    )
```

```python
import jax
import jax.numpy as jnp
from jax import lax
from jax.experimental import pallas as pl
from jax.experimental.pallas import tpu as pltpu
from jax.sharding import PartitionSpec as P

ITERS = 5
beta_stat = 0.6
damping = 0.75

NC = 2
INTERPRET = False

f32 = jnp.float32
bf16 = jnp.bfloat16
HI = lax.Precision.HIGHEST


def inverse_root(matrix):
    size = matrix.shape[0]
    eye = jnp.eye(size, dtype=matrix.dtype)
    sym = 0.5 * (matrix + matrix.T) + damping * eye
    scale = jnp.sqrt(jnp.sum(sym * sym))
    current = sym / scale
    result = eye
    for sweep in range(ITERS):
        factor = (5.0 * eye - current) * 0.25
        if sweep == 0:
            result = factor
        else:
            result = jnp.dot(result, factor, precision=HI)
        if sweep < ITERS - 1:
            square = jnp.dot(factor, factor, precision=HI)
            fourth = jnp.dot(square, square, precision=HI)
            current = jnp.dot(fourth, current, precision=HI)
    return result * scale ** (-0.25)


def exchange(x, axis, groups=None):
    return lax.all_to_all(x, axis, 0, 0, axis_index_groups=groups, tiled=True)


def tables(pattern, holders, position, held, n_dp):
    rows, cols = pattern[:, 0], pattern[:, 1]
    entries = jnp.arange(holders.shape[0], dtype=jnp.int32)
    off = rows != cols
    same = (holders[None, :] == holders[:, None]) & (entries[None, :] < entries[:, None])
    within = jnp.sum(same.astype(jnp.int32), axis=1)
    rank = jnp.sum((same & off[None, :]).astype(jnp.int32), axis=1)
    dests = jnp.arange(n_dp, dtype=jnp.int32)
    mine = off[None, :] & (holders[None, :] == dests[:, None])
    needs = [dests, dests]
    for m in range(held - 1):
        hit = (mine & (rank[None, :] == m)).astype(jnp.int32)
        needs.append(jnp.sum(hit * rows[None, :], axis=1))
        needs.append(jnp.sum(hit * cols[None, :], axis=1))
    diag_slot = jnp.sum(jnp.where((~off) & (holders == position), within, 0))
    return needs, diag_slot


def regroup(x, low_two, even):
    v0, v1, v2, v3 = x[0], x[1], x[2], x[3]
    a0, a2 = jnp.where(low_two, v0, pltpu.roll(v2, 4, 1)), jnp.where(low_two, pltpu.roll(v0, 4, 1), v2)
    a1, a3 = jnp.where(low_two, v1, pltpu.roll(v3, 4, 1)), jnp.where(low_two, pltpu.roll(v1, 4, 1), v3)
    b0, b1 = jnp.where(even, a0, pltpu.roll(a1, 2, 1)), jnp.where(even, pltpu.roll(a0, 6, 1), a1)
    b2, b3 = jnp.where(even, a2, pltpu.roll(a3, 2, 1)), jnp.where(even, pltpu.roll(a2, 6, 1), a3)
    return b0, b1, b2, b3


def combine_kernel(core, keep_a, keep_b, got_a, got_b, out):
    tiles, width = got_a.shape[1] // 8, got_a.shape[2]
    sub = lax.broadcasted_iota(jnp.int32, (tiles, 8, width), 1)
    low_two, even = sub < 4, jnp.bitwise_and(sub, 2) == 0
    for chunk, (keep, got) in enumerate(((keep_a, got_a), (keep_b, got_b))):
        groups = [
            regroup(
                (keep[g : g + 4] + got[g : g + 4]).reshape(4, tiles, 8, width), low_two, even
            )
            for g in (0, 4)
        ]
        for j in range(4):
            both = jnp.concatenate([groups[0][j], groups[1][j]], axis=1).astype(bf16)
            out[:, j, chunk] = both


def combine(core, part_a, part_b, got_a, got_b):
    panels, rows, width = got_a.shape
    keep_spec = pl.BlockSpec((8, None, rows, width), lambda i, core: (i, core[0], 0, 0))
    got_spec = pl.BlockSpec((8, rows, width), lambda i, core: (i, 0, 0))
    return pl.pallas_call(
        combine_kernel,
        out_shape=jax.ShapeDtypeStruct((rows // 8, 4, 2, 2 * panels, width), bf16),
        grid_spec=pltpu.PrefetchScalarGridSpec(
            num_scalar_prefetch=1,
            grid=(panels // 8,),
            in_specs=[keep_spec, keep_spec, got_spec, got_spec],
            out_specs=pl.BlockSpec((rows // 8, 4, 2, 16, width), lambda i, core: (0, 0, 0, i, 0)),
        ),
        cost_estimate=pl.CostEstimate(
            flops=2 * panels * rows * width, bytes_accessed=20 * panels * rows * width, transcendentals=0
        ),
        compiler_params=pltpu.CompilerParams(vmem_limit_bytes=8 << 20),
        interpret=INTERPRET,
    )(core.reshape(1), part_a, part_b, got_a, got_b)


def per_device(activations, out_grads, stat_old, pattern, holders):
    position = lax.axis_index("dp")
    stat_pos = lax.axis_index("stat")
    n_stat = lax.axis_size("stat")
    n_dp = lax.axis_size("dp")
    places = n_dp // NC
    block = stat_old.shape[2]
    held = stat_old.shape[0]
    width = out_grads.shape[1]
    rows = activations.shape[1]
    panels = rows // block
    half = block // NC
    share = block // n_stat
    core = jnp.bitwise_and(position, NC - 1)

    def product(chunk):
        partial = lax.dot_general(
            activations[:, chunk * (rows // 2) : (chunk + 1) * (rows // 2)],
            out_grads,
            (((0,), (0,)), ((), ())),
            preferred_element_type=f32,
        ).reshape(panels // 2, NC, half, width)
        give = jnp.where(core == 0, partial[:, 1], partial[:, 0])
        return partial, lax.ppermute(give, "dp", [(i, i ^ 1) for i in range(n_dp)])

    part_a, got_a = product(0)
    part_b, got_b = product(1)
    pair = combine(core, part_a, part_b, got_a, got_b).reshape(places, 2 * panels, width)
    groups = [[NC * j + c for j in range(places)] for c in range(NC)]
    owned = jnp.sum(exchange(pair, "dp", groups).astype(f32), axis=0)

    needs, diag_slot = tables(pattern, holders, position, held, n_dp)
    kinds = len(needs)
    padded = 8
    wanted = 2 * jnp.stack(needs, axis=1)[:, :, None] + jnp.arange(2)
    wanted = wanted + 2 * panels * (jnp.arange(kinds) == 1).astype(jnp.int32)[:, None]
    wanted = jnp.pad(wanted, ((0, 0), (0, padded - kinds), (0, 0)), constant_values=-1)
    pick = wanted.reshape(-1, 1) == jnp.arange(4 * panels, dtype=jnp.int32)
    high = lax.reduce_precision(owned, 8, 7)
    source = jnp.concatenate([high, owned - high]).astype(bf16)
    sent = jnp.dot(pick.astype(bf16), source, preferred_element_type=f32).astype(bf16)
    came = exchange(sent.reshape(n_dp, 2 * padded, width), "dp")
    came = came.reshape(places, NC, padded, 2, width).transpose(2, 1, 0, 3, 4)
    came = came.reshape(padded, block, width)

    def gram_of(a, b):
        return lax.dot_general(a, b, (((1,), (1,)), ((), ())), preferred_element_type=f32)

    diag = jnp.broadcast_to(gram_of(came[0], came[0])[None], (n_stat, block, block))
    others = [
        gram_of(came[2 + 2 * m], came[3 + 2 * m]).reshape(n_stat, share, block)
        for m in range(held - 1)
    ]
    grams = exchange(jnp.concatenate([diag] + others, axis=1), "stat")
    grams = jnp.sum(grams, axis=0) * ((1.0 - beta_stat) / (width * n_stat))

    old_diag = lax.dynamic_index_in_dim(stat_old, diag_slot, 0, keepdims=False)
    new_diag = beta_stat * old_diag + grams[:block]
    root = inverse_root(new_diag)
    grad = came[0].astype(f32) + came[1].astype(f32)
    direction = jnp.dot(root, grad, precision=HI)

    diag_rows = lax.dynamic_slice_in_dim(grams[:block], stat_pos * share, share, 0)
    slots = []
    for j in range(held):
        part = diag_rows
        for m in range(held - 1):
            here = (diag_slot != j) & (jnp.where(diag_slot < j, j - 1, j) == m)
            part = jnp.where(here, grams[block + m * share : block + (m + 1) * share], part)
        slots.append(part)
    old_rows = lax.dynamic_slice_in_dim(stat_old, stat_pos * share, share, 1)
    statistics = beta_stat * old_rows + jnp.stack(slots)
    return (direction, statistics)


def solution(mesh):
    placed = (P("dp", None), P("dp", "stat"), P("dp", None, None), P(), P())
    return jax.shard_map(
        per_device,
        mesh=mesh,
        in_specs=placed,
        out_specs=(P("dp", "stat"), P("dp", "stat", None)),
        check_vma=False,
    )
```

```python
import functools

import jax
import jax.numpy as jnp
from jax import lax
from jax.experimental import pallas as pl
from jax.experimental.pallas import tpu as pltpu
from jax.sharding import PartitionSpec as P

ITERS = 5
beta_stat = 0.6
damping = 0.75

NY, NC = 4, 2
INTERPRET = False

f32 = jnp.float32
bf16 = jnp.bfloat16
HI = lax.Precision.HIGHEST


def exchange(x, axis, groups=None):
    return lax.all_to_all(x, axis, 0, 0, axis_index_groups=groups, tiled=True)


def tables(pattern, holders, position, held, n_dp):
    rows, cols = pattern[:, 0], pattern[:, 1]
    entries = jnp.arange(holders.shape[0], dtype=jnp.int32)
    off = rows != cols
    same = (holders[None, :] == holders[:, None]) & (entries[None, :] < entries[:, None])
    within = jnp.sum(same.astype(jnp.int32), axis=1)
    rank = jnp.sum((same & off[None, :]).astype(jnp.int32), axis=1)
    dests = jnp.arange(n_dp, dtype=jnp.int32)
    mine = off[None, :] & (holders[None, :] == dests[:, None])
    needs = [dests, dests]
    for m in range(held - 1):
        hit = (mine & (rank[None, :] == m)).astype(jnp.int32)
        needs.append(jnp.sum(hit * rows[None, :], axis=1))
        needs.append(jnp.sum(hit * cols[None, :], axis=1))
    diag_slot = jnp.sum(jnp.where((~off) & (holders == position), within, 0))
    return needs, diag_slot


def regroup(x, low_two, even):
    v0, v1, v2, v3 = x[0], x[1], x[2], x[3]
    a0, a2 = jnp.where(low_two, v0, pltpu.roll(v2, 4, 1)), jnp.where(low_two, pltpu.roll(v0, 4, 1), v2)
    a1, a3 = jnp.where(low_two, v1, pltpu.roll(v3, 4, 1)), jnp.where(low_two, pltpu.roll(v1, 4, 1), v3)
    b0, b1 = jnp.where(even, a0, pltpu.roll(a1, 2, 1)), jnp.where(even, pltpu.roll(a0, 6, 1), a1)
    b2, b3 = jnp.where(even, a2, pltpu.roll(a3, 2, 1)), jnp.where(even, pltpu.roll(a2, 6, 1), a3)
    return b0, b1, b2, b3


def combine_kernel(keep_a, keep_b, got_a, got_b, out):
    tiles, width = got_a.shape[1] // 8, got_a.shape[2]
    sub = lax.broadcasted_iota(jnp.int32, (tiles, 8, width), 1)
    low_two, even = sub < 4, jnp.bitwise_and(sub, 2) == 0
    for chunk, (keep, got) in enumerate(((keep_a, got_a), (keep_b, got_b))):
        groups = [
            regroup(
                (keep[g : g + 4] + got[g : g + 4].astype(f32)).reshape(4, tiles, 8, width),
                low_two,
                even,
            )
            for g in (0, 4)
        ]
        for j in range(4):
            both = jnp.concatenate([groups[0][j], groups[1][j]], axis=1).astype(bf16)
            out[:, j, chunk] = both


def combine(keep_a, keep_b, got_a, got_b):
    panels, rows, width = got_a.shape
    spec = pl.BlockSpec((8, rows, width), lambda i: (i, 0, 0))
    return pl.pallas_call(
        combine_kernel,
        out_shape=jax.ShapeDtypeStruct((rows // 8, 4, 2, 2 * panels, width), bf16),
        grid=(panels // 8,),
        in_specs=[spec] * 4,
        out_specs=pl.BlockSpec((rows // 8, 4, 2, 16, width), lambda i: (0, 0, 0, i, 0)),
        cost_estimate=pl.CostEstimate(
            flops=2 * panels * rows * width, bytes_accessed=16 * panels * rows * width, transcendentals=0
        ),
        compiler_params=pltpu.CompilerParams(vmem_limit_bytes=8 << 20),
        interpret=INTERPRET,
    )(keep_a, keep_b, got_a, got_b)


def split_kernel(where, part, got, give, keep):
    x = (part[...] + got[...]).reshape(got.shape[0], got.shape[1] // 16, 2, 8, got.shape[2])
    even, odd = x[:, :, 0].reshape(give.shape), x[:, :, 1].reshape(give.shape)
    mine_even = where[1] == 0
    give[...] = jnp.where(mine_even, odd, even).astype(bf16)
    keep[...] = jnp.where(mine_even, even, odd)


def split(where, part, got):
    panels, rows, width = got.shape
    step = 8
    out_spec = pl.BlockSpec((step, rows // 2, width), lambda i, where: (i, 0, 0))
    return pl.pallas_call(
        split_kernel,
        out_shape=[
            jax.ShapeDtypeStruct((panels, rows // 2, width), bf16),
            jax.ShapeDtypeStruct((panels, rows // 2, width), f32),
        ],
        grid_spec=pltpu.PrefetchScalarGridSpec(
            num_scalar_prefetch=1,
            grid=(panels // step,),
            in_specs=[
                pl.BlockSpec((step, None, rows, width), lambda i, where: (i, where[0], 0, 0)),
                pl.BlockSpec((step, rows, width), lambda i, where: (i, 0, 0)),
            ],
            out_specs=[out_spec, out_spec],
        ),
        cost_estimate=pl.CostEstimate(
            flops=panels * rows * width, bytes_accessed=11 * panels * rows * width, transcendentals=0
        ),
        compiler_params=pltpu.CompilerParams(vmem_limit_bytes=8 << 20),
        interpret=INTERPRET,
    )(where, part, got)


def dot_hi(a, b):
    return jnp.dot(a, b, precision=HI, preferred_element_type=f32)


def finish_kernel(where, grams, old_diag, old_rows, high, low, direction, statistics, *, scale):
    slot, pos = where[0], where[1]
    block = old_diag.shape[0]
    held, share = old_rows.shape[0], old_rows.shape[1]
    total = grams[0]
    for i in range(1, grams.shape[0]):
        total = total + grams[i]
    total = total * scale
    row = lax.broadcasted_iota(jnp.int32, (block, block), 0)
    eye = jnp.where(row == lax.broadcasted_iota(jnp.int32, (block, block), 1), 1.0, 0.0)
    new = beta_stat * old_diag[...] + total[:block]
    sym = 0.5 * (new + new.T) + damping * eye
    norm = jnp.sqrt(jnp.sum(jnp.sum(sym * sym, axis=1, keepdims=True), axis=0, keepdims=True))
    current = sym / norm
    result = None
    for sweep in range(ITERS):
        factor = (5.0 * eye - current) * 0.25
        result = factor if sweep == 0 else dot_hi(result, factor)
        if sweep < ITERS - 1:
            square = dot_hi(factor, factor)
            fourth = dot_hi(square, square)
            current = dot_hi(fourth, current)
    root = result / jnp.sqrt(jnp.sqrt(norm))
    direction[...] = dot_hi(root, high[...].astype(f32) + low[...].astype(f32))
    diag = jnp.zeros((share, block), f32)
    for p in range(block // share):
        diag = diag + jnp.where(pos == p, total[p * share : (p + 1) * share], 0.0)
    for j in range(held):
        part = diag
        for m in range(held - 1):
            at = m + jnp.where(slot <= m, 1, 0)
            part = jnp.where(at == j, total[block + m * share : block + (m + 1) * share], part)
        statistics[j] = beta_stat * old_rows[j] + part


def finish(where, grams, old_diag, old_rows, high, low, scale):
    block, width = high.shape
    vmem = pl.BlockSpec(memory_space=pltpu.VMEM)
    return pl.pallas_call(
        functools.partial(finish_kernel, scale=scale),
        out_shape=[
            jax.ShapeDtypeStruct((block, width), f32),
            jax.ShapeDtypeStruct(old_rows.shape, f32),
        ],
        in_specs=[pl.BlockSpec(memory_space=pltpu.SMEM)] + [vmem] * 5,
        out_specs=[vmem, vmem],
        compiler_params=pltpu.CompilerParams(vmem_limit_bytes=16 << 20),
        interpret=INTERPRET,
    )(where, grams, old_diag, old_rows, high, low)


def per_device(activations, out_grads, stat_old, pattern, holders):
    position = lax.axis_index("dp")
    stat_pos = lax.axis_index("stat")
    n_stat = lax.axis_size("stat")
    n_dp = lax.axis_size("dp")
    places = n_dp // NC
    block = stat_old.shape[2]
    held = stat_old.shape[0]
    width = out_grads.shape[1]
    rows = activations.shape[1]
    panels = rows // block
    half = block // NC
    share = block // n_stat
    core = jnp.bitwise_and(position, NC - 1)

    def product(chunk):
        partial = lax.dot_general(
            activations[:, chunk * (rows // 2) : (chunk + 1) * (rows // 2)],
            out_grads,
            (((0,), (0,)), ((), ())),
            preferred_element_type=f32,
        ).reshape(panels // 2, NC, half, width)
        give = jnp.where(core == 0, partial[:, 1], partial[:, 0])
        return partial, lax.ppermute(give, "dp", [(i, i ^ 1) for i in range(n_dp)])

    part_a, got_a = product(0)
    part_b, got_b = product(1)
    neighbour = NY * NC
    where = jnp.stack([core, jnp.bitwise_and(position // neighbour, 1)])
    swap = [(i, i ^ neighbour) for i in range(n_dp)]
    give_a, keep_a = split(where, part_a, got_a)
    got_a = lax.ppermute(give_a, "dp", swap)
    give_b, keep_b = split(where, part_b, got_b)
    got_b = lax.ppermute(give_b, "dp", swap)
    pair = combine(keep_a, keep_b, got_a, got_b).reshape(places // 2, 2 * panels, width)
    groups = [
        [(2 * q + p) * neighbour + y * NC + c for q in range(places // (2 * NY)) for y in range(NY)]
        for p in range(2)
        for c in range(NC)
    ]
    owned = jnp.sum(exchange(pair, "dp", groups).astype(f32), axis=0)

    needs, diag_slot = tables(pattern, holders, position, held, n_dp)
    kinds = len(needs)
    padded = 8
    wanted = 2 * jnp.stack(needs, axis=1)[:, :, None] + jnp.arange(2)
    wanted = wanted + 2 * panels * (jnp.arange(kinds) == 1).astype(jnp.int32)[:, None]
    wanted = jnp.pad(wanted, ((0, 0), (0, padded - kinds), (0, 0)), constant_values=-1)
    pick = wanted.reshape(-1, 1) == jnp.arange(4 * panels, dtype=jnp.int32)
    high = lax.reduce_precision(owned, 8, 7)
    source = jnp.concatenate([high, owned - high]).astype(bf16)
    sent = jnp.dot(pick.astype(bf16), source, preferred_element_type=f32).astype(bf16)
    came = exchange(sent.reshape(n_dp, 2 * padded, width), "dp")
    came = came.reshape(places, NC, padded, 2, width).transpose(2, 1, 0, 3, 4)
    came = came.reshape(padded, block, width)

    def gram_of(a, b):
        return lax.dot_general(a, b, (((1,), (1,)), ((), ())), preferred_element_type=f32)

    diag = jnp.broadcast_to(gram_of(came[0], came[0])[None], (n_stat, block, block))
    others = [
        gram_of(came[2 + 2 * m], came[3 + 2 * m]).reshape(n_stat, share, block)
        for m in range(held - 1)
    ]
    grams = exchange(jnp.concatenate([diag] + others, axis=1), "stat")
    old_diag = lax.dynamic_index_in_dim(stat_old, diag_slot, 0, keepdims=False)
    old_rows = lax.dynamic_slice_in_dim(stat_old, stat_pos * share, share, 1)
    place = jnp.stack([diag_slot, stat_pos]).astype(jnp.int32)
    scale = (1.0 - beta_stat) / (width * n_stat)
    direction, statistics = finish(place, grams, old_diag, old_rows, came[0], came[1], scale)
    return (direction, statistics)


def solution(mesh):
    placed = (P("dp", None), P("dp", "stat"), P("dp", None, None), P(), P())
    return jax.shard_map(
        per_device,
        mesh=mesh,
        in_specs=placed,
        out_specs=(P("dp", "stat"), P("dp", "stat", None)),
        check_vma=False,
    )
```

```python
import functools

import jax
import jax.numpy as jnp
from jax import lax
from jax.experimental import pallas as pl
from jax.experimental.pallas import tpu as pltpu
from jax.sharding import PartitionSpec as P

ITERS = 5
beta_stat = 0.6
damping = 0.75

NC = 2
INTERPRET = False

f32 = jnp.float32
bf16 = jnp.bfloat16
HI = lax.Precision.HIGHEST


def exchange(x, axis, groups=None):
    return lax.all_to_all(x, axis, 0, 0, axis_index_groups=groups, tiled=True)


def tables(pattern, holders, position, held, n_dp):
    rows, cols = pattern[:, 0], pattern[:, 1]
    entries = jnp.arange(holders.shape[0], dtype=jnp.int32)
    off = rows != cols
    same = (holders[None, :] == holders[:, None]) & (entries[None, :] < entries[:, None])
    within = jnp.sum(same.astype(jnp.int32), axis=1)
    rank = jnp.sum((same & off[None, :]).astype(jnp.int32), axis=1)
    dests = jnp.arange(n_dp, dtype=jnp.int32)
    mine = off[None, :] & (holders[None, :] == dests[:, None])
    needs = [dests, dests]
    for m in range(held - 1):
        hit = (mine & (rank[None, :] == m)).astype(jnp.int32)
        needs.append(jnp.sum(hit * rows[None, :], axis=1))
        needs.append(jnp.sum(hit * cols[None, :], axis=1))
    diag_slot = jnp.sum(jnp.where((~off) & (holders == position), within, 0))
    return needs, diag_slot


def regroup(x, low_two, even):
    v0, v1, v2, v3 = x[0], x[1], x[2], x[3]
    a0, a2 = jnp.where(low_two, v0, pltpu.roll(v2, 4, 1)), jnp.where(low_two, pltpu.roll(v0, 4, 1), v2)
    a1, a3 = jnp.where(low_two, v1, pltpu.roll(v3, 4, 1)), jnp.where(low_two, pltpu.roll(v1, 4, 1), v3)
    b0, b1 = jnp.where(even, a0, pltpu.roll(a1, 2, 1)), jnp.where(even, pltpu.roll(a0, 6, 1), a1)
    b2, b3 = jnp.where(even, a2, pltpu.roll(a3, 2, 1)), jnp.where(even, pltpu.roll(a2, 6, 1), a3)
    return b0, b1, b2, b3


def combine_kernel(core, keep_a, keep_b, got_a, got_b, out):
    tiles, width = got_a.shape[1] // 8, got_a.shape[2]
    sub = lax.broadcasted_iota(jnp.int32, (tiles, 8, width), 1)
    low_two, even = sub < 4, jnp.bitwise_and(sub, 2) == 0
    for chunk, (keep, got) in enumerate(((keep_a, got_a), (keep_b, got_b))):
        groups = [
            regroup(
                (keep[g : g + 4] + got[g : g + 4]).reshape(4, tiles, 8, width), low_two, even
            )
            for g in (0, 4)
        ]
        for j in range(4):
            both = jnp.concatenate([groups[0][j], groups[1][j]], axis=1).astype(bf16)
            out[:, j, chunk] = both


def combine(core, part_a, part_b, got_a, got_b):
    panels, rows, width = got_a.shape
    keep_spec = pl.BlockSpec((8, None, rows, width), lambda i, core: (i, core[0], 0, 0))
    got_spec = pl.BlockSpec((8, rows, width), lambda i, core: (i, 0, 0))
    return pl.pallas_call(
        combine_kernel,
        out_shape=jax.ShapeDtypeStruct((rows // 8, 4, 2, 2 * panels, width), bf16),
        grid_spec=pltpu.PrefetchScalarGridSpec(
            num_scalar_prefetch=1,
            grid=(panels // 8,),
            in_specs=[keep_spec, keep_spec, got_spec, got_spec],
            out_specs=pl.BlockSpec((rows // 8, 4, 2, 16, width), lambda i, core: (0, 0, 0, i, 0)),
        ),
        cost_estimate=pl.CostEstimate(
            flops=2 * panels * rows * width, bytes_accessed=20 * panels * rows * width, transcendentals=0
        ),
        compiler_params=pltpu.CompilerParams(vmem_limit_bytes=8 << 20),
        interpret=INTERPRET,
    )(core.reshape(1), part_a, part_b, got_a, got_b)


def dot_hi(a, b):
    return jnp.dot(a, b, precision=HI, preferred_element_type=f32)


def finish_kernel(where, came, old_diag, old_rows, high, low, direction, statistics, *, scale):
    slot, pos = where[0], where[1]
    block = old_diag.shape[0]
    held, share = old_rows.shape[0], old_rows.shape[1]
    diag_gram = jnp.zeros((block, block), f32)
    rest = jnp.zeros((came.shape[1] - block, block), f32)
    for i in range(came.shape[0]):
        panel = came[i, :block]
        diag_gram = diag_gram + lax.dot_general(
            panel, panel, (((1,), (1,)), ((), ())), preferred_element_type=f32
        )
        rest = rest + came[i, block:].astype(f32)
    diag_gram, rest = diag_gram * scale, rest * scale
    row = lax.broadcasted_iota(jnp.int32, (block, block), 0)
    eye = jnp.where(row == lax.broadcasted_iota(jnp.int32, (block, block), 1), 1.0, 0.0)
    new = beta_stat * old_diag[...] + diag_gram
    sym = 0.5 * (new + new.T) + damping * eye
    norm = jnp.sqrt(jnp.sum(jnp.sum(sym * sym, axis=1, keepdims=True), axis=0, keepdims=True))
    current = sym / norm
    result = None
    for sweep in range(ITERS):
        factor = (5.0 * eye - current) * 0.25
        result = factor if sweep == 0 else dot_hi(result, factor)
        if sweep < ITERS - 1:
            square = dot_hi(factor, factor)
            fourth = dot_hi(square, square)
            current = dot_hi(fourth, current)
    root = result / jnp.sqrt(jnp.sqrt(norm))
    direction[...] = dot_hi(root, high[...].astype(f32) + low[...].astype(f32))
    diag = jnp.zeros((share, block), f32)
    for p in range(block // share):
        diag = diag + jnp.where(pos == p, diag_gram[p * share : (p + 1) * share], 0.0)
    for j in range(held):
        part = diag
        for m in range(held - 1):
            at = m + jnp.where(slot <= m, 1, 0)
            part = jnp.where(at == j, rest[m * share : (m + 1) * share], part)
        statistics[j] = beta_stat * old_rows[j] + part


def finish(where, came, old_diag, old_rows, high, low, scale):
    block, width = high.shape
    vmem = pl.BlockSpec(memory_space=pltpu.VMEM)
    return pl.pallas_call(
        functools.partial(finish_kernel, scale=scale),
        out_shape=[
            jax.ShapeDtypeStruct((block, width), f32),
            jax.ShapeDtypeStruct(old_rows.shape, f32),
        ],
        in_specs=[pl.BlockSpec(memory_space=pltpu.SMEM)] + [vmem] * 5,
        out_specs=[vmem, vmem],
        compiler_params=pltpu.CompilerParams(vmem_limit_bytes=16 << 20),
        interpret=INTERPRET,
    )(where, came, old_diag, old_rows, high, low)


def per_device(activations, out_grads, stat_old, pattern, holders):
    position = lax.axis_index("dp")
    stat_pos = lax.axis_index("stat")
    n_stat = lax.axis_size("stat")
    n_dp = lax.axis_size("dp")
    places = n_dp // NC
    block = stat_old.shape[2]
    held = stat_old.shape[0]
    width = out_grads.shape[1]
    rows = activations.shape[1]
    panels = rows // block
    half = block // NC
    share = block // n_stat
    core = jnp.bitwise_and(position, NC - 1)

    def product(chunk):
        partial = lax.dot_general(
            activations[:, chunk * (rows // 2) : (chunk + 1) * (rows // 2)],
            out_grads,
            (((0,), (0,)), ((), ())),
            preferred_element_type=f32,
        ).reshape(panels // 2, NC, half, width)
        give = jnp.where(core == 0, partial[:, 1], partial[:, 0])
        return partial, lax.ppermute(give, "dp", [(i, i ^ 1) for i in range(n_dp)])

    part_a, got_a = product(0)
    part_b, got_b = product(1)
    pair = combine(core, part_a, part_b, got_a, got_b).reshape(places, 2 * panels, width)
    groups = [[NC * j + c for j in range(places)] for c in range(NC)]
    owned = jnp.sum(exchange(pair, "dp", groups).astype(f32), axis=0)

    needs, diag_slot = tables(pattern, holders, position, held, n_dp)
    old_diag = lax.dynamic_index_in_dim(stat_old, diag_slot, 0, keepdims=False)
    old_rows = lax.dynamic_slice_in_dim(stat_old, stat_pos * share, share, 1)
    place = jnp.stack([diag_slot, stat_pos]).astype(jnp.int32)
    owned, old_diag, old_rows, place = lax.optimization_barrier((owned, old_diag, old_rows, place))
    kinds = len(needs)
    padded = 8
    wanted = 2 * jnp.stack(needs, axis=1)[:, :, None] + jnp.arange(2)
    wanted = wanted + 2 * panels * (jnp.arange(kinds) == 1).astype(jnp.int32)[:, None]
    wanted = jnp.pad(wanted, ((0, 0), (0, padded - kinds), (0, 0)), constant_values=-1)
    pick = wanted.reshape(-1, 1) == jnp.arange(4 * panels, dtype=jnp.int32)
    high = lax.reduce_precision(owned, 8, 7)
    source = jnp.concatenate([high, owned - high]).astype(bf16)
    sent = jnp.dot(pick.astype(bf16), source, preferred_element_type=f32).astype(bf16)
    came = exchange(sent.reshape(n_dp, 2 * padded, width), "dp")
    came = came.reshape(places, NC, padded, 2, width).transpose(2, 1, 0, 3, 4)
    came = came.reshape(padded, block, width)

    def gram_of(a, b):
        return lax.dot_general(a, b, (((1,), (1,)), ((), ())), preferred_element_type=f32)

    own = jnp.broadcast_to(came[0][None], (n_stat, block, width))
    others = [
        gram_of(came[2 + 2 * m], came[3 + 2 * m]).astype(bf16).reshape(n_stat, share, block)
        for m in range(held - 1)
    ]
    gathered = exchange(jnp.concatenate([own] + others, axis=1), "stat")
    scale = (1.0 - beta_stat) / (width * n_stat)
    direction, statistics = finish(place, gathered, old_diag, old_rows, came[0], came[1], scale)
    return (direction, statistics)


def solution(mesh):
    placed = (P("dp", None), P("dp", "stat"), P("dp", None, None), P(), P())
    return jax.shard_map(
        per_device,
        mesh=mesh,
        in_specs=placed,
        out_specs=(P("dp", "stat"), P("dp", "stat", None)),
        check_vma=False,
    )
```
